256 devices in a mesh: lat: 8 (over z_hi, y), lon: 32 (over z_lo, x, core).
Axes of the slice: x: 4, y: 4, z: 8 (z_hi: 2, z_lo: 4; z = z_hi * 4 + z_lo), core: 2. Of those that a mesh axis runs over, the one named last changes fastest.
Arguments:
- species_amounts: float32 [32, 128, 32, 128], P('lat', 'lon'), may hold values from 0.1 to 3
- thermal_anomaly: float32 [32, 128, 32], P('lat', 'lon'), may hold values from -1 to 1
- solar_flux_factor: float32 [32, 128], P('lat', 'lon'), may hold values from 0 to 1
- inner_iterations: int32 [32, 128], P('lat', 'lon'), may hold values from 4 to 36
- reference_speed: float32 [512], replicated, may hold values from 0.01 to 3
- thermal_response: float32 [512], replicated, may hold values from -1 to 1
- photo_breakup: float32 [512], replicated, may hold values from 0.03 to 3
- reaction_recipe: int32 [4, 512], replicated, may hold values from 0 to 127
- eastward_wind_ratio: float32 [32, 32, 128], P('lon', 'lat'), may hold values from -0.95 to 0.95
- northward_wind_ratio: float32 [32, 32, 128], P('lon', 'lat'), may hold values from -0.95 to 0.95
Outputs:
- transported: float32 [32, 128, 32, 128], P('lat', 'lon')
The draws below stay inside these ranges and needn't reach their ends.
Inputs may be any that keep to these rules, and one draw needn't show every extreme that they name: `reaction_recipe`: row 0 and row 1 name the two reactants of each reaction, rows 2 and 3 its two products.
All inputs are finite; a program needn't handle non-finite values.
Results may differ from the reference program's by a relative error of at most 0.0003.
Values sent between devices are 32-bit elements; how exact they have to be, the bound alone decides.
No kernel may reach another device: no remote copies, remote signals or barrier semaphores. Data moves between devices by JAX's collectives and lax.ppermute only.
A program may use at most 64 MiB of HBM per device.

```python
import math
import jax
import jax.numpy as jnp
from jax import lax

S = 128
R = 512
MINSUB = 4
MAXSUB = 36
ADV_STEPS = 2
PARALLEL_TOTAL = 32
MERIDIAN_TOTAL = 128
ALTITUDE_LAYERS = 32


def draw_inner_iterations(key, part):
    dawn_key = jax.random.fold_in(key, 11)
    day_key = jax.random.fold_in(key, 12)
    night_key = jax.random.fold_in(key, 13)
    dawn_lon = jax.random.randint(dawn_key, (), 0, MERIDIAN_TOTAL)
    longitude = lax.broadcasted_iota(jnp.int32, (PARALLEL_TOTAL, MERIDIAN_TOTAL), 1)
    distance = (longitude - dawn_lon) % MERIDIAN_TOTAL
    sunlit = distance < MERIDIAN_TOTAL // 2
    day_count = jax.random.randint(day_key, (PARALLEL_TOTAL, MERIDIAN_TOTAL), 24, MAXSUB + 1)
    night_count = jax.random.randint(night_key, (PARALLEL_TOTAL, MERIDIAN_TOTAL), MINSUB, MINSUB + 3)
    counts = jnp.where(sunlit, day_count, night_count)
    counts = counts.at[0, dawn_lon].set(MAXSUB)
    counts = counts.at[0, (dawn_lon + MERIDIAN_TOTAL // 2) % MERIDIAN_TOTAL].set(MINSUB)
    return counts.astype(jnp.int32)


def place_ends(values, own_key, least, top_value):
    spot = [jax.random.randint(jax.random.fold_in(own_key, axis), (), 0, length) for axis, length in enumerate(values.shape)]
    longest = values.shape.index(max(values.shape))
    beside = spot[:longest] + [(spot[longest] + 1) % values.shape[longest]] + spot[longest + 1:]
    return values.at[tuple(spot)].set(least).at[tuple(beside)].set(top_value)


def block_levels(rng, dims, pieces, low, largest):
    loudness = 1.0
    for position, shards_of in pieces:
        steps = jax.random.uniform(jax.random.fold_in(jax.random.fold_in(rng, 6), position), (shards_of,), jnp.float32, low / len(pieces), largest / len(pieces))
        loudness = loudness * jnp.repeat(jnp.exp(steps), dims[position] // shards_of).reshape((-1,) + (1,) * (len(dims) - 1 - position))
    return loudness


def setup_inputs(seed: int = 0) -> dict:
    streams_of = jax.random.split(jax.random.key(seed), 11)
    species_amounts = jnp.clip(jnp.exp(math.log(3.0) - 3.4011974 * jax.random.uniform(streams_of[0], (PARALLEL_TOTAL, MERIDIAN_TOTAL, ALTITUDE_LAYERS, S), jnp.float32) ** block_levels(streams_of[0], (PARALLEL_TOTAL, MERIDIAN_TOTAL, ALTITUDE_LAYERS, S), ((0, 8), (1, 32)), -0.2, 0.2)), 0.1, 3.0)
    thermal_anomaly = jnp.clip(jax.random.uniform(streams_of[1], (PARALLEL_TOTAL, MERIDIAN_TOTAL, ALTITUDE_LAYERS), jnp.float32, -1.0, 1.0) * block_levels(streams_of[1], (PARALLEL_TOTAL, MERIDIAN_TOTAL, ALTITUDE_LAYERS), ((0, 8), (1, 32)), -0.4, 0.0), -1.0, 1.0)
    solar_flux_factor = jnp.clip(1.0 * jax.random.uniform(streams_of[2], (PARALLEL_TOTAL, MERIDIAN_TOTAL), jnp.float32) ** block_levels(streams_of[2], (PARALLEL_TOTAL, MERIDIAN_TOTAL), ((0, 8), (1, 32)), -0.2, 0.2), 0.0, 1.0)
    inner_iterations = draw_inner_iterations(jax.random.fold_in(streams_of[10], 71), 0)
    reference_speed = jnp.clip(jnp.exp(jax.random.uniform(streams_of[4], (R,), jnp.float32, math.log(0.01), math.log(3.0))), 0.01, 3.0)
    thermal_response = jnp.clip(jax.random.uniform(streams_of[5], (R,), jnp.float32, -1.0, 1.0), -1.0, 1.0)
    photo_breakup = jnp.clip(jnp.exp(jax.random.uniform(streams_of[6], (R,), jnp.float32, math.log(0.03), math.log(3.0))), 0.03, 3.0)
    reaction_recipe = place_ends(jax.random.randint(streams_of[7], (4, R), 0, S), jax.random.fold_in(streams_of[7], 1), 0, S - 1).astype(jnp.int32)
    eastward_wind_ratio = jnp.clip(jax.random.uniform(streams_of[8], (ALTITUDE_LAYERS, PARALLEL_TOTAL, MERIDIAN_TOTAL), jnp.float32, -0.95, 0.95) * block_levels(streams_of[8], (ALTITUDE_LAYERS, PARALLEL_TOTAL, MERIDIAN_TOTAL), ((0, 32), (1, 8)), -0.4, 0.0), -0.95, 0.95)
    northward_wind_ratio = jnp.clip(jax.random.uniform(streams_of[9], (ALTITUDE_LAYERS, PARALLEL_TOTAL, MERIDIAN_TOTAL), jnp.float32, -0.95, 0.95) * block_levels(streams_of[9], (ALTITUDE_LAYERS, PARALLEL_TOTAL, MERIDIAN_TOTAL), ((0, 32), (1, 8)), -0.4, 0.0), -0.95, 0.95)
    return {"species_amounts": species_amounts, "thermal_anomaly": thermal_anomaly, "solar_flux_factor": solar_flux_factor, "inner_iterations": inner_iterations, "reference_speed": reference_speed, "thermal_response": thermal_response, "photo_breakup": photo_breakup, "reaction_recipe": reaction_recipe, "eastward_wind_ratio": eastward_wind_ratio, "northward_wind_ratio": northward_wind_ratio}


def slice_axis(array, start, count, along):
    return lax.slice_in_dim(array, start, start + count, axis=along)


def flux_sweep(padded, courant_pad, along, length):
    far_left = slice_axis(padded, 0, length + 3, along)
    near_left = slice_axis(padded, 1, length + 3, along)
    near_right = slice_axis(padded, 2, length + 3, along)
    far_right = slice_axis(padded, 3, length + 3, along)
    edges = (7.0 / 12.0) * (near_left + near_right) - (1.0 / 12.0) * (far_left + far_right)
    edges = jnp.minimum(jnp.maximum(edges, jnp.minimum(near_left, near_right)), jnp.maximum(near_left, near_right))
    cell_means = slice_axis(padded, 2, length + 2, along)
    left_edge = slice_axis(edges, 0, length + 2, along)
    right_edge = slice_axis(edges, 1, length + 2, along)
    edge_jump = right_edge - left_edge
    curvature = 6.0 * cell_means - 3.0 * (left_edge + right_edge)
    courant = slice_axis(courant_pad, 3, length + 1, along)
    magnitude = jnp.abs(courant)
    from_left = slice_axis(right_edge, 0, length + 1, along) - 0.5 * courant * (
        slice_axis(edge_jump, 0, length + 1, along)
        - (1.0 - (2.0 / 3.0) * courant) * slice_axis(curvature, 0, length + 1, along))
    from_right = slice_axis(left_edge, 1, length + 1, along) + 0.5 * magnitude * (
        slice_axis(edge_jump, 1, length + 1, along)
        + (1.0 - (2.0 / 3.0) * magnitude) * slice_axis(curvature, 1, length + 1, along))
    face_flux = courant * jnp.where(courant >= 0.0, from_left, from_right)
    interior = slice_axis(padded, 3, length, along)
    return interior - (slice_axis(face_flux, 1, length, along) - slice_axis(face_flux, 0, length, along))


def wrap_pad(array, along):
    extent = array.shape[along]
    return jnp.concatenate([slice_axis(array, extent - 3, 3, along), array, slice_axis(array, 0, 3, along)], axis=along)


def zero_pad(array, along):
    widths = [(0, 0)] * array.ndim
    widths[along] = (3, 3)
    return jnp.pad(array, widths)


def reference(species_amounts, thermal_anomaly, solar_flux_factor, inner_iterations, reference_speed, thermal_response, photo_breakup, reaction_recipe, eastward_wind_ratio, northward_wind_ratio):
    species = species_amounts.shape[-1]

    def lone_parallel(inputs):
        conc_row, warmth_strip, sun_row, count_row = inputs
        local_warmth = warmth_strip.reshape(1, -1)
        local_irradiance = jnp.broadcast_to(sun_row[:, None], warmth_strip.shape).reshape(1, -1)
        speed_coefficient = reference_speed[:, None] * jnp.exp(thermal_response[:, None] * local_warmth) + photo_breakup[:, None] * local_irradiance
        mesh_box_total = jnp.broadcast_to(count_row[:, None], warmth_strip.shape).reshape(1, -1)
        substep = 1.0 / mesh_box_total.astype(jnp.float32)
        start = conc_row.reshape(-1, species).T

        def advance(step_index, current):
            first_conc = current[reaction_recipe[0]]
            second_conc = current[reaction_recipe[1]]
            reaction_flow = speed_coefficient * first_conc * second_conc
            produced = jax.ops.segment_sum(reaction_flow, reaction_recipe[2], species) + jax.ops.segment_sum(reaction_flow, reaction_recipe[3], species)
            lost_rate = jax.ops.segment_sum(speed_coefficient * second_conc, reaction_recipe[0], species) + jax.ops.segment_sum(speed_coefficient * first_conc, reaction_recipe[1], species)
            updated = (current + substep * produced) / (1.0 + substep * lost_rate)
            return jnp.where(step_index < mesh_box_total, updated, current)

        result = lax.fori_loop(0, MAXSUB, advance, start)
        return result.T.reshape(conc_row.shape)

    carried_quantity = lax.map(lone_parallel, (species_amounts, thermal_anomaly, solar_flux_factor, inner_iterations))
    east_faces = jnp.transpose(eastward_wind_ratio, (1, 2, 0))[..., None]
    row_ids = lax.broadcasted_iota(jnp.int32, (carried_quantity.shape[0], 1, 1, 1), 0)
    south_faces = jnp.where(row_ids > 0, jnp.transpose(northward_wind_ratio, (1, 2, 0))[..., None], 0.0)
    east_pad = wrap_pad(east_faces, 1)
    south_pad = zero_pad(south_faces, 0)
    for sweep_index in range(ADV_STEPS):
        carried_quantity = flux_sweep(wrap_pad(carried_quantity, 1), east_pad, 1, carried_quantity.shape[1])
        carried_quantity = flux_sweep(zero_pad(carried_quantity, 0), south_pad, 0, carried_quantity.shape[0])
    return carried_quantity
```

```python
import functools

import jax
import jax.numpy as jnp
from jax import lax
from jax.experimental import pallas as pl
from jax.experimental.pallas import tpu as pltpu
from jax.sharding import PartitionSpec as P

ADV_STEPS = 2
LANES = 16
FLOOR = 1e-30
GROUP = 8
UNROLL = 2
SHUFFLED = 1
PARTS = 2
INPUTS = 8
BF = jnp.bfloat16
F32 = jnp.float32
VMEM = pl.BlockSpec(memory_space=pltpu.VMEM)
SMEM = pl.BlockSpec(memory_space=pltpu.SMEM)


def store_parts(refs, at, value):
    size = value.shape[0] // len(refs)
    for part, ref in enumerate(refs):
        ref[at] = value[part * size : (part + 1) * size]


def load_parts(refs, at):
    return jnp.concatenate([ref[at] for ref in refs], axis=0)


def one_hot(row, size):
    ids = lax.broadcasted_iota(jnp.int32, (size, row.shape[1]), 0)
    return (jnp.broadcast_to(row, ids.shape) == ids).astype(F32)


def split_halves(value):
    high = value.astype(BF)
    return high, (value - high.astype(F32)).astype(BF)


def pack_winds(eastward, northward, rows, turned, packed):
    n_lat, n_lon = eastward.shape[1:]
    owners = packed.shape[0]
    own = n_lon // owners
    rows[...] = jnp.zeros_like(rows)
    rows[:n_lat, :] = eastward[0]
    first = lax.broadcasted_iota(jnp.int32, (n_lat, n_lon), 0) + lax.axis_index("lat") == 0
    rows[n_lat : 2 * n_lat, :] = jnp.where(first, 0.0, northward[0])
    turned[...] = rows[...].T
    pieces = [turned[pl.ds(i, owners, stride=own), :] for i in range(own)]
    pieces.append(jnp.concatenate([pieces[0][1:], pieces[0][:1]], axis=0))
    total = pieces[0]
    for i in range(1, own + 1):
        total = total + pltpu.roll(pieces[i], LANES * i, axis=1)
    packed[:, 0, :] = total


def chemistry_kernel(
    counts, solar, *refs, group
):
    sources, outputs = refs[:INPUTS], refs[INPUTS : INPUTS + 2 + 2 * PARTS]
    settled, packed = outputs[:2]
    to_east, to_west = outputs[2 : 2 + PARTS], outputs[2 + PARTS :]
    refs = refs[INPUTS + 2 + 2 * PARTS :]
    held, (order, rates, state, sums, gather, square, turned, waiting, arrived) = (
        refs[:INPUTS], refs[INPUTS:]
    )
    copies = [
        pltpu.make_async_copy(source, target, arrived.at[i])
        for i, (source, target) in enumerate(zip(sources, held))
    ]
    for copy in copies:
        copy.start()
    recipe, eastward, northward, speed, response, photo, warmth, species = held
    n_lat, n_lon, levels, kinds = species.shape
    reactions = recipe.shape[1]
    columns = n_lat * n_lon
    chunks = reactions // 128

    flat = [counts[i // n_lon, i % n_lon] for i in range(columns)]
    for i in range(columns):
        rank = jnp.int32(0)
        for j in range(columns):
            if j != i:
                ahead = flat[j] >= flat[i] if j < i else flat[j] > flat[i]
                rank = rank + ahead.astype(jnp.int32)
        order[rank] = i

    def place(slot):
        column = order[slot]
        return column // n_lon, lax.rem(column, n_lon)

    def count_of(slot):
        a, b = place(slot)
        return counts[a, b]

    for copy in copies:
        copy.wait()
    pack_winds(eastward, northward, square, turned, packed)

    for chunk in range(chunks):
        lanes = slice(chunk * 128, (chunk + 1) * 128)
        first, second, third, fourth = [one_hot(recipe[r : r + 1, lanes], kinds) for r in range(4)]
        both = jnp.concatenate([first, second], axis=1).astype(BF)
        gather[chunk, :kinds, :] = both
        gather[chunk, kinds:, :] = both
        ends = jnp.concatenate([(third + fourth).T, (first + second).T], axis=1).astype(BF)
        sums[chunk * 256 : chunk * 256 + 128, :] = ends
        sums[chunk * 256 + 128 : chunk * 256 + 256, :] = ends

    for i in range(columns):
        a, b = place(i)
        square[i : i + 1, :levels] = warmth[a, pl.ds(b, 1), :]
    warm_columns = square[...].T
    exponent, base, light = response[...], speed[...], photo[...]
    for i in range(columns):
        a, b = place(i)
        rows = slice(i * levels, (i + 1) * levels)
        warm = jnp.broadcast_to(warm_columns[:levels, i : i + 1], (levels, reactions))
        rates[rows, :] = base * jnp.exp(exponent * warm) + light * solar[a, b]
        state[rows, :] = jnp.maximum(species[a, b], FLOOR)

    def sums_of(start, length):
        rows = slice(start * levels, (start + length) * levels)
        amounts = state[rows, :]
        picked = jnp.concatenate(split_halves(amounts), axis=1)
        flows = []
        for chunk in range(chunks):
            lanes = slice(chunk * 128, (chunk + 1) * 128)
            if chunk < chunks - SHUFFLED:
                pair = jnp.dot(picked, gather[chunk], preferred_element_type=F32)
                first, second = pair[:, :128], pair[:, 128:]
            else:
                first, second = [
                    jnp.take_along_axis(
                        amounts,
                        jnp.broadcast_to(recipe[r : r + 1, lanes], amounts.shape),
                        axis=1,
                        mode="promise_in_bounds",
                    )
                    for r in range(2)
                ]
            flows.extend(split_halves(rates[rows, lanes] * first * second))
        return jnp.dot(jnp.concatenate(flows, axis=1), sums[...], preferred_element_type=F32)

    def update(start, length, both, t, ns, steps):
        for i in range(length):
            rows = slice((start + i) * levels, (start + i + 1) * levels)
            part = slice(i * levels, (i + 1) * levels)
            amount, n, step = state[rows, :], ns[start + i], steps[start + i]
            grown = amount + step * both[part, :kinds]
            kept = amount / (amount + step * both[part, kinds:])
            state[rows, :] = jnp.where(t < n, jnp.maximum(grown * kept, FLOOR), amount)

    def run(live, begin, trips):
        half = live // 2
        ns = [count_of(i) for i in range(live)]
        steps = [1.0 / n.astype(F32) for n in ns]
        rows = slice(0, half * levels)

        @pl.when(trips > 0)
        def _():
            waiting[rows, :] = sums_of(half, half)

            def substeps(trip, carry):
                held = waiting[rows, :]
                for offset in range(UNROLL):
                    t = begin + trip * UNROLL + offset
                    both = sums_of(0, half)
                    update(half, half, held, t, ns, steps)
                    held = sums_of(half, half)
                    update(0, half, both, t, ns, steps)
                waiting[rows, :] = held
                return carry

            lax.fori_loop(0, trips, substeps, 0)

    begin = jnp.int32(0)
    for live in range(columns, 0, -group):
        trips = jnp.maximum(count_of(live - group) - begin + UNROLL - 1, 0) // UNROLL
        run(live, begin, trips)
        begin = begin + trips * UNROLL

    for i in range(columns):
        a, b = place(i)
        value = state[i * levels : (i + 1) * levels, :]
        settled[a, b] = value

        @pl.when(b > 0)
        def _():
            store_parts(to_east, (a, jnp.maximum(b - 1, 0)), value)

        @pl.when(b < n_lon - 1)
        def _():
            store_parts(to_west, (a, jnp.minimum(b, n_lon - 2)), value)


def chemistry(counts, solar, *arrays):
    recipe, eastward, species = arrays[0], arrays[1], arrays[-1]
    n_lat, n_lon, levels, kinds = species.shape
    reactions, longitudes = recipe.shape[1], eastward.shape[2]
    columns = n_lat * n_lon
    halo = jax.ShapeDtypeStruct((n_lat, n_lon - 1, levels // PARTS, kinds), F32)
    return pl.pallas_call(
        functools.partial(chemistry_kernel, group=GROUP),
        out_shape=(
            jax.ShapeDtypeStruct(species.shape, F32),
            jax.ShapeDtypeStruct((longitudes // n_lon, 1, 128), F32),
        )
        + (halo,) * (2 * PARTS),
        in_specs=[SMEM, SMEM] + [pl.BlockSpec(memory_space=pltpu.HBM)] * INPUTS,
        out_specs=(VMEM,) * (2 + 2 * PARTS),
        scratch_shapes=[pltpu.VMEM(array.shape, array.dtype) for array in arrays]
        + [
            pltpu.SMEM((columns,), jnp.int32),
            pltpu.VMEM((columns * levels, reactions), F32),
            pltpu.VMEM((columns * levels, kinds), F32),
            pltpu.VMEM((2 * reactions, 2 * kinds), BF),
            pltpu.VMEM((reactions // 128, 2 * kinds, 256), BF),
            pltpu.VMEM((128, 128), F32),
            pltpu.VMEM((128, 128), F32),
            pltpu.VMEM((columns * levels // 2, 2 * kinds), F32),
            pltpu.SemaphoreType.DMA((INPUTS,)),
        ],
        compiler_params=pltpu.CompilerParams(vmem_limit_bytes=62 << 20),
        cost_estimate=pl.CostEstimate(
            flops=int(2e10), bytes_accessed=2 << 20, transcendentals=0
        ),
        name="chemistry",
    )(counts, solar, *arrays)


def sweep_line(cells, faces):
    count = len(cells) - 6
    edges = {}
    for k in range(2, count + 5):
        far_left, left, right, far_right = cells[k - 2 : k + 2]
        edge = (7.0 / 12.0) * (left + right) - (1.0 / 12.0) * (far_left + far_right)
        edges[k] = jnp.minimum(
            jnp.maximum(edge, jnp.minimum(left, right)), jnp.maximum(left, right)
        )
    jumps, curves = {}, {}
    for k in range(2, count + 4):
        jumps[k] = edges[k + 1] - edges[k]
        curves[k] = 6.0 * cells[k] - 3.0 * (edges[k] + edges[k + 1])
    flux = []
    for k in range(count + 1):
        courant, at = faces[k], k + 3
        size = jnp.abs(courant)
        upwind = courant >= 0.0
        jump = jnp.where(upwind, -jumps[at - 1], jumps[at])
        curve = jnp.where(upwind, curves[at - 1], curves[at])
        value = edges[at] + 0.5 * size * (jump + (1.0 - (2.0 / 3.0) * size) * curve)
        flux.append(courant * value)
    return [cells[k + 3] - (flux[k + 1] - flux[k]) for k in range(count)]


def spread(wind, lane, tile):
    return jnp.broadcast_to(wind[:, lane : lane + 1], tile)


def wind_rows(wind, rows):
    for i in range(rows.shape[0]):
        rows[i : i + 1, :] = wind[i]
    return rows[...]


def zonal_kernel(block, wind, *refs):
    low, high = refs[:PARTS], refs[PARTS : 2 * PARTS]
    swept, inner, outer, rows = refs[2 * PARTS :]
    n_lat, n_lon = block.shape[:2]
    tile = block.shape[2:]
    winds = wind_rows(wind, rows)
    even = lax.rem(lax.axis_index("lat"), 2) == 0
    inner[(n_lat - 1) * n_lon] = winds
    outer[(n_lat - 1) * n_lon] = winds
    lines = []
    for a in range(n_lat):
        cells = [load_parts(low, (a, i)) for i in range(3)]
        cells += [block[a, i] for i in range(n_lon)]
        cells += [load_parts(high, (a, i)) for i in range(3)]
        faces = [spread(winds, LANES * k + a, tile) for k in range(n_lon + 1)]
        lines.append(sweep_line(cells, faces))
        for i, value in enumerate(lines[a]):
            swept[a, i] = value
            if a > 0:
                at, below = (a - 1) * n_lon + i, lines[a - 1][i]
                inner[at] = jnp.where(even, value, below)
                outer[at] = jnp.where(even, below, value)


def meridional_kernel(block, wind, inner, outer, swept, *refs):
    *sends, rows = refs
    n_lat, n_lon = block.shape[:2]
    tile = block.shape[2:]
    band = lax.axis_index("lat")
    even = lax.rem(band, 2) == 0
    south_end, north_end = band == 0, band == lax.axis_size("lat") - 1

    def low(at):
        return jnp.where(south_end, 0.0, jnp.where(even, outer[at], inner[at]))

    def high(at):
        return jnp.where(north_end, 0.0, jnp.where(even, inner[at], outer[at]))

    winds, above = wind_rows(wind, rows), high(3 * n_lon)
    for i in range(n_lon):
        cells = [low(a * n_lon + i) for a in range(3)]
        cells += [block[a, i] for a in range(n_lat)]
        cells += [high(a * n_lon + i) for a in range(3)]
        faces = [spread(winds, LANES * i + n_lat + k, tile) for k in range(n_lat)]
        faces.append(spread(above, LANES * i + n_lat, tile))
        for a, value in enumerate(sweep_line(cells, faces)):
            swept[a, i] = value
            if sends and i > 0:
                store_parts(sends[:PARTS], (a, i - 1), value)
            if sends and i < n_lon - 1:
                store_parts(sends[PARTS:], (a, i), value)


def sweep(kernel, block, wind, halos, sent_shapes, name):
    shapes = (block.shape,) + sent_shapes
    return pl.pallas_call(
        kernel,
        out_shape=tuple(jax.ShapeDtypeStruct(shape, F32) for shape in shapes),
        in_specs=[VMEM] * (2 + len(halos)),
        out_specs=(VMEM,) * len(shapes),
        scratch_shapes=[pltpu.VMEM((wind.shape[0], wind.shape[2]), F32)],
        compiler_params=pltpu.CompilerParams(vmem_limit_bytes=24 << 20),
        name=name,
    )(block, wind, *halos)


def per_device(
    species_amounts,
    thermal_anomaly,
    solar_flux_factor,
    inner_iterations,
    reference_speed,
    thermal_response,
    photo_breakup,
    reaction_recipe,
    eastward_wind_ratio,
    northward_wind_ratio,
):
    n_lat, n_lon, levels, kinds = species_amounts.shape
    lon_count, lat_count = lax.axis_size("lon"), lax.axis_size("lat")
    eastbound = [(i, (i + 1) % lon_count) for i in range(lon_count)]
    westbound = [(target, source) for source, target in eastbound]
    inner_pairs = [(i, i ^ 1) for i in range(lat_count)]
    outer_pairs = [(i, min(max(((i + 1) ^ 1) - 1, 0), lat_count - 1)) for i in range(lat_count)]

    block, packed, *sends = chemistry(
        inner_iterations,
        solar_flux_factor,
        reaction_recipe,
        eastward_wind_ratio,
        northward_wind_ratio,
        reference_speed[None],
        thermal_response[None],
        photo_breakup[None],
        thermal_anomaly,
        species_amounts,
    )
    wind = lax.all_to_all(packed, "lon", split_axis=0, concat_axis=0, tiled=True)
    zonal_halo = (n_lat, n_lon - 1, levels // PARTS, kinds)
    meridional_halo = ((n_lat - 1) * n_lon + 1, levels, kinds)
    for step in range(ADV_STEPS):
        halos = [
            lax.ppermute(sent, "lon", eastbound if i < PARTS else westbound)
            for i, sent in enumerate(sends)
        ]
        block, inner, outer = sweep(
            zonal_kernel, block, wind, halos, (meridional_halo,) * 2, "zonal"
        )
        outer = lax.ppermute(outer, "lat", outer_pairs)
        inner = lax.ppermute(inner, "lat", inner_pairs)
        last = step == ADV_STEPS - 1
        sent_shapes = () if last else (zonal_halo,) * (2 * PARTS)
        block, *sends = sweep(
            meridional_kernel, block, wind, (inner, outer), sent_shapes, "meridional"
        )
    return block


def solution(mesh):
    return jax.shard_map(
        per_device,
        mesh=mesh,
        in_specs=(
            P("lat", "lon", None, None),
            P("lat", "lon", None),
            P("lat", "lon"),
            P("lat", "lon"),
            P(),
            P(),
            P(),
            P(),
            P("lon", "lat", None),
            P("lon", "lat", None),
        ),
        out_specs=P("lat", "lon", None, None),
        check_vma=False,
    )
```

```python
import functools

import jax
import jax.numpy as jnp
from jax import lax
from jax.experimental import pallas as pl
from jax.experimental.pallas import tpu as pltpu
from jax.sharding import PartitionSpec as P

ADV_STEPS = 2
LANES = 16
FLOOR = 1e-30
GROUP = 8
UNROLL = 4
SHUFFLED = 1
PARTS = 2
INPUTS = 8
BF = jnp.bfloat16
F32 = jnp.float32
VMEM = pl.BlockSpec(memory_space=pltpu.VMEM)
SMEM = pl.BlockSpec(memory_space=pltpu.SMEM)


def store_parts(refs, at, value):
    size = value.shape[0] // len(refs)
    for part, ref in enumerate(refs):
        ref[at] = value[part * size : (part + 1) * size]


def load_parts(refs, at):
    return jnp.concatenate([ref[at] for ref in refs], axis=0)


def one_hot(row, size):
    ids = lax.broadcasted_iota(jnp.int32, (size, row.shape[1]), 0)
    return (jnp.broadcast_to(row, ids.shape) == ids).astype(F32)


def split_halves(value):
    high = value.astype(BF)
    return high, (value - high.astype(F32)).astype(BF)


def pack_winds(eastward, northward, rows, turned, packed):
    n_lat, n_lon = eastward.shape[1:]
    owners = packed.shape[0]
    own = n_lon // owners
    rows[...] = jnp.zeros_like(rows)
    rows[:n_lat, :] = eastward[0]
    first = lax.broadcasted_iota(jnp.int32, (n_lat, n_lon), 0) + lax.axis_index("lat") == 0
    rows[n_lat : 2 * n_lat, :] = jnp.where(first, 0.0, northward[0])
    turned[...] = rows[...].T
    pieces = [turned[pl.ds(i, owners, stride=own), :] for i in range(own)]
    pieces.append(jnp.concatenate([pieces[0][1:], pieces[0][:1]], axis=0))
    total = pieces[0]
    for i in range(1, own + 1):
        total = total + pltpu.roll(pieces[i], LANES * i, axis=1)
    packed[:, 0, :] = total


def chemistry_kernel(
    counts, solar, *refs, group
):
    sources, outputs = refs[:INPUTS], refs[INPUTS : INPUTS + 2 + 2 * PARTS]
    settled, packed = outputs[:2]
    to_east, to_west = outputs[2 : 2 + PARTS], outputs[2 + PARTS :]
    refs = refs[INPUTS + 2 + 2 * PARTS :]
    held, (order, rates, state, sums, gather, square, turned, waiting, arrived) = (
        refs[:INPUTS], refs[INPUTS:]
    )
    copies = [
        pltpu.make_async_copy(source, target, arrived.at[i])
        for i, (source, target) in enumerate(zip(sources, held))
    ]
    for copy in copies:
        copy.start()
    recipe, eastward, northward, speed, response, photo, warmth, species = held
    n_lat, n_lon, levels, kinds = species.shape
    reactions = recipe.shape[1]
    columns = n_lat * n_lon
    chunks = reactions // 128

    flat = [counts[i // n_lon, i % n_lon] for i in range(columns)]
    for i in range(columns):
        rank = jnp.int32(0)
        for j in range(columns):
            if j != i:
                ahead = flat[j] >= flat[i] if j < i else flat[j] > flat[i]
                rank = rank + ahead.astype(jnp.int32)
        order[rank] = i

    def place(slot):
        column = order[slot]
        return column // n_lon, lax.rem(column, n_lon)

    def count_of(slot):
        a, b = place(slot)
        return counts[a, b]

    for copy in copies:
        copy.wait()
    pack_winds(eastward, northward, square, turned, packed)

    for chunk in range(chunks):
        lanes = slice(chunk * 128, (chunk + 1) * 128)
        first, second, third, fourth = [one_hot(recipe[r : r + 1, lanes], kinds) for r in range(4)]
        both = jnp.concatenate([first, second], axis=1).astype(BF)
        gather[chunk, :kinds, :] = both
        gather[chunk, kinds:, :] = both
        ends = jnp.concatenate([(third + fourth).T, (first + second).T], axis=1).astype(BF)
        sums[chunk * 256 : chunk * 256 + 128, :] = ends
        sums[chunk * 256 + 128 : chunk * 256 + 256, :] = ends

    for i in range(columns):
        a, b = place(i)
        square[i : i + 1, :levels] = warmth[a, pl.ds(b, 1), :]
    warm_columns = square[...].T
    exponent, base, light = response[...], speed[...], photo[...]
    for i in range(columns):
        a, b = place(i)
        rows = slice(i * levels, (i + 1) * levels)
        warm = jnp.broadcast_to(warm_columns[:levels, i : i + 1], (levels, reactions))
        rates[rows, :] = base * jnp.exp(exponent * warm) + light * solar[a, b]
        state[rows, :] = jnp.maximum(species[a, b], FLOOR)

    def sums_of(start, length):
        rows = slice(start * levels, (start + length) * levels)
        amounts = state[rows, :]
        picked = jnp.concatenate(split_halves(amounts), axis=1)
        flows = []
        for chunk in range(chunks):
            lanes = slice(chunk * 128, (chunk + 1) * 128)
            if chunk < chunks - SHUFFLED:
                pair = jnp.dot(picked, gather[chunk], preferred_element_type=F32)
                first, second = pair[:, :128], pair[:, 128:]
            else:
                first, second = [
                    jnp.take_along_axis(
                        amounts,
                        jnp.broadcast_to(recipe[r : r + 1, lanes], amounts.shape),
                        axis=1,
                        mode="promise_in_bounds",
                    )
                    for r in range(2)
                ]
            flows.extend(split_halves(rates[rows, lanes] * first * second))
        return jnp.dot(jnp.concatenate(flows, axis=1), sums[...], preferred_element_type=F32)

    def update(start, length, both, t, ns, steps):
        for i in range(length):
            rows = slice((start + i) * levels, (start + i + 1) * levels)
            part = slice(i * levels, (i + 1) * levels)
            amount, n, step = state[rows, :], ns[start + i], steps[start + i]
            grown = amount + step * both[part, :kinds]
            kept = amount / (amount + step * both[part, kinds:])
            state[rows, :] = jnp.where(t < n, jnp.maximum(grown * kept, FLOOR), amount)

    def run(live, begin, trips):
        half = live // 2
        ns = [count_of(i) for i in range(live)]
        steps = [1.0 / n.astype(F32) for n in ns]
        rows = slice(0, half * levels)

        @pl.when(trips > 0)
        def _():
            waiting[rows, :] = sums_of(half, half)

            def substeps(trip, carry):
                held = waiting[rows, :]
                for offset in range(UNROLL):
                    t = begin + trip * UNROLL + offset
                    both = sums_of(0, half)
                    update(half, half, held, t, ns, steps)
                    held = sums_of(half, half)
                    update(0, half, both, t, ns, steps)
                waiting[rows, :] = held
                return carry

            lax.fori_loop(0, trips, substeps, 0)

    begin = jnp.int32(0)
    for live in range(columns, 0, -group):
        trips = jnp.maximum(count_of(live - group) - begin + UNROLL - 1, 0) // UNROLL
        run(live, begin, trips)
        begin = begin + trips * UNROLL

    for i in range(columns):
        a, b = place(i)
        value = state[i * levels : (i + 1) * levels, :]
        settled[a, b] = value

        @pl.when(b > 0)
        def _():
            store_parts(to_east, (a, jnp.maximum(b - 1, 0)), value)

        @pl.when(b < n_lon - 1)
        def _():
            store_parts(to_west, (a, jnp.minimum(b, n_lon - 2)), value)


def chemistry(counts, solar, *arrays):
    recipe, eastward, species = arrays[0], arrays[1], arrays[-1]
    n_lat, n_lon, levels, kinds = species.shape
    reactions, longitudes = recipe.shape[1], eastward.shape[2]
    columns = n_lat * n_lon
    halo = pltpu.VMEM((n_lat, n_lon - 1, levels // PARTS, kinds), F32)
    return pl.pallas_call(
        functools.partial(chemistry_kernel, group=GROUP),
        out_shape=(
            pltpu.VMEM(species.shape, F32),
            jax.ShapeDtypeStruct((longitudes // n_lon, 1, 128), F32),
        )
        + (halo,) * (2 * PARTS),
        in_specs=[SMEM, SMEM] + [pl.BlockSpec(memory_space=pltpu.HBM)] * INPUTS,
        out_specs=(VMEM,) * (2 + 2 * PARTS),
        scratch_shapes=[pltpu.VMEM(array.shape, array.dtype) for array in arrays]
        + [
            pltpu.SMEM((columns,), jnp.int32),
            pltpu.VMEM((columns * levels, reactions), F32),
            pltpu.VMEM((columns * levels, kinds), F32),
            pltpu.VMEM((2 * reactions, 2 * kinds), BF),
            pltpu.VMEM((reactions // 128, 2 * kinds, 256), BF),
            pltpu.VMEM((128, 128), F32),
            pltpu.VMEM((128, 128), F32),
            pltpu.VMEM((columns * levels // 2, 2 * kinds), F32),
            pltpu.SemaphoreType.DMA((INPUTS,)),
        ],
        compiler_params=pltpu.CompilerParams(vmem_limit_bytes=60 << 20),
        cost_estimate=pl.CostEstimate(
            flops=int(2e10), bytes_accessed=2 << 20, transcendentals=0
        ),
        name="chemistry",
    )(counts, solar, *arrays)


def sweep_line(cells, faces):
    count = len(cells) - 6
    edges = {}
    for k in range(2, count + 5):
        far_left, left, right, far_right = cells[k - 2 : k + 2]
        edge = (7.0 / 12.0) * (left + right) - (1.0 / 12.0) * (far_left + far_right)
        edges[k] = jnp.minimum(
            jnp.maximum(edge, jnp.minimum(left, right)), jnp.maximum(left, right)
        )
    jumps, curves = {}, {}
    for k in range(2, count + 4):
        jumps[k] = edges[k + 1] - edges[k]
        curves[k] = 6.0 * cells[k] - 3.0 * (edges[k] + edges[k + 1])
    flux = []
    for k in range(count + 1):
        courant, at = faces[k], k + 3
        size = jnp.abs(courant)
        upwind = courant >= 0.0
        jump = jnp.where(upwind, -jumps[at - 1], jumps[at])
        curve = jnp.where(upwind, curves[at - 1], curves[at])
        value = edges[at] + 0.5 * size * (jump + (1.0 - (2.0 / 3.0) * size) * curve)
        flux.append(courant * value)
    return [cells[k + 3] - (flux[k + 1] - flux[k]) for k in range(count)]


def spread(wind, lane, tile):
    return jnp.broadcast_to(wind[:, lane : lane + 1], tile)


def wind_rows(wind, rows):
    for i in range(rows.shape[0]):
        rows[i : i + 1, :] = wind[i]
    return rows[...]


def zonal_kernel(block, wind, *refs):
    low, high = refs[:PARTS], refs[PARTS : 2 * PARTS]
    swept, inner, outer, rows = refs[2 * PARTS :]
    n_lat, n_lon = block.shape[:2]
    tile = block.shape[2:]
    winds = wind_rows(wind, rows)
    even = lax.rem(lax.axis_index("lat"), 2) == 0
    inner[(n_lat - 1) * n_lon] = winds
    outer[(n_lat - 1) * n_lon] = winds
    lines = []
    for a in range(n_lat):
        cells = [load_parts(low, (a, i)) for i in range(3)]
        cells += [block[a, i] for i in range(n_lon)]
        cells += [load_parts(high, (a, i)) for i in range(3)]
        faces = [spread(winds, LANES * k + a, tile) for k in range(n_lon + 1)]
        lines.append(sweep_line(cells, faces))
        for i, value in enumerate(lines[a]):
            swept[a, i] = value
            if a > 0:
                at, below = (a - 1) * n_lon + i, lines[a - 1][i]
                inner[at] = jnp.where(even, value, below)
                outer[at] = jnp.where(even, below, value)


def meridional_kernel(block, wind, outer, inner, swept, *refs):
    *sends, rows = refs
    n_lat, n_lon = block.shape[:2]
    tile = block.shape[2:]
    band = lax.axis_index("lat")
    even = lax.rem(band, 2) == 0
    south_end, north_end = band == 0, band == lax.axis_size("lat") - 1

    def low(at):
        return jnp.where(south_end, 0.0, jnp.where(even, outer[at], inner[at]))

    def high(at):
        return jnp.where(north_end, 0.0, jnp.where(even, inner[at], outer[at]))

    winds, above = wind_rows(wind, rows), high(3 * n_lon)
    for i in range(n_lon):
        cells = [low(a * n_lon + i) for a in range(3)]
        cells += [block[a, i] for a in range(n_lat)]
        cells += [high(a * n_lon + i) for a in range(3)]
        faces = [spread(winds, LANES * i + n_lat + k, tile) for k in range(n_lat)]
        faces.append(spread(above, LANES * i + n_lat, tile))
        for a, value in enumerate(sweep_line(cells, faces)):
            swept[a, i] = value
            if sends and i > 0:
                store_parts(sends[:PARTS], (a, i - 1), value)
            if sends and i < n_lon - 1:
                store_parts(sends[PARTS:], (a, i), value)


def sweep(kernel, block, wind, halos, sent_shapes, name):
    shapes = (block.shape,) + sent_shapes
    return pl.pallas_call(
        kernel,
        out_shape=tuple(jax.ShapeDtypeStruct(shape, F32) for shape in shapes),
        in_specs=[VMEM] * (2 + len(halos)),
        out_specs=(VMEM,) * len(shapes),
        scratch_shapes=[pltpu.VMEM((wind.shape[0], wind.shape[2]), F32)],
        compiler_params=pltpu.CompilerParams(vmem_limit_bytes=24 << 20),
        name=name,
    )(block, wind, *halos)


def per_device(
    species_amounts,
    thermal_anomaly,
    solar_flux_factor,
    inner_iterations,
    reference_speed,
    thermal_response,
    photo_breakup,
    reaction_recipe,
    eastward_wind_ratio,
    northward_wind_ratio,
):
    n_lat, n_lon, levels, kinds = species_amounts.shape
    lon_count, lat_count = lax.axis_size("lon"), lax.axis_size("lat")
    eastbound = [(i, (i + 1) % lon_count) for i in range(lon_count)]
    westbound = [(target, source) for source, target in eastbound]
    inner_pairs = [(i, i ^ 1) for i in range(lat_count)]
    outer_pairs = [(i, min(max(((i + 1) ^ 1) - 1, 0), lat_count - 1)) for i in range(lat_count)]

    block, packed, *sends = chemistry(
        inner_iterations,
        solar_flux_factor,
        reaction_recipe,
        eastward_wind_ratio,
        northward_wind_ratio,
        reference_speed[None],
        thermal_response[None],
        photo_breakup[None],
        thermal_anomaly,
        species_amounts,
    )
    wind = lax.all_to_all(packed, "lon", split_axis=0, concat_axis=0, tiled=True)
    zonal_halo = (n_lat, n_lon - 1, levels // PARTS, kinds)
    meridional_halo = ((n_lat - 1) * n_lon + 1, levels, kinds)
    for step in range(ADV_STEPS):
        halos = [
            lax.ppermute(sent, "lon", eastbound if i < PARTS else westbound)
            for i, sent in enumerate(sends)
        ]
        block, inner, outer = sweep(
            zonal_kernel, block, wind, halos, (meridional_halo,) * 2, "zonal"
        )
        inner = lax.ppermute(inner, "lat", inner_pairs)
        outer = lax.ppermute(outer, "lat", outer_pairs)
        last = step == ADV_STEPS - 1
        sent_shapes = () if last else (zonal_halo,) * (2 * PARTS)
        block, *sends = sweep(
            meridional_kernel, block, wind, (outer, inner), sent_shapes, "meridional"
        )
    return block


def solution(mesh):
    return jax.shard_map(
        per_device,
        mesh=mesh,
        in_specs=(
            P("lat", "lon", None, None),
            P("lat", "lon", None),
            P("lat", "lon"),
            P("lat", "lon"),
            P(),
            P(),
            P(),
            P(),
            P("lon", "lat", None),
            P("lon", "lat", None),
        ),
        out_specs=P("lat", "lon", None, None),
        check_vma=False,
    )
```

```python
import functools

import jax
import jax.numpy as jnp
from jax import lax
from jax.experimental import pallas as pl
from jax.experimental.pallas import tpu as pltpu
from jax.sharding import PartitionSpec as P

ADV_STEPS = 2
LANES = 16
FLOOR = 1e-30
GROUP = 8
UNROLL = 4
SHUFFLED = 1
PARTS = 2
INPUTS = 8
BF = jnp.bfloat16
F32 = jnp.float32
VMEM = pl.BlockSpec(memory_space=pltpu.VMEM)
SMEM = pl.BlockSpec(memory_space=pltpu.SMEM)


def store_parts(refs, at, value):
    size = value.shape[0] // len(refs)
    for part, ref in enumerate(refs):
        ref[at] = value[part * size : (part + 1) * size]


def load_parts(refs, at):
    return jnp.concatenate([ref[at] for ref in refs], axis=0)


def one_hot(row, size):
    ids = lax.broadcasted_iota(jnp.int32, (size, row.shape[1]), 0)
    return (jnp.broadcast_to(row, ids.shape) == ids).astype(F32)


def split_halves(value):
    high = value.astype(BF)
    return high, (value - high.astype(F32)).astype(BF)


def pack_winds(eastward, northward, rows, turned, packed):
    n_lat, n_lon = eastward.shape[1:]
    owners = packed.shape[0]
    own = n_lon // owners
    rows[...] = jnp.zeros_like(rows)
    rows[:n_lat, :] = eastward[0]
    first = lax.broadcasted_iota(jnp.int32, (n_lat, n_lon), 0) + lax.axis_index("lat") == 0
    rows[n_lat : 2 * n_lat, :] = jnp.where(first, 0.0, northward[0])
    turned[...] = rows[...].T
    pieces = [turned[pl.ds(i, owners, stride=own), :] for i in range(own)]
    pieces.append(jnp.concatenate([pieces[0][1:], pieces[0][:1]], axis=0))
    total = pieces[0]
    for i in range(1, own + 1):
        total = total + pltpu.roll(pieces[i], LANES * i, axis=1)
    packed[:, 0, :] = total


def chemistry_kernel(
    counts, solar, *refs, group
):
    sources, outputs = refs[:INPUTS], refs[INPUTS : INPUTS + 2 + 2 * PARTS]
    settled, packed = outputs[:2]
    to_east, to_west = outputs[2 : 2 + PARTS], outputs[2 + PARTS :]
    refs = refs[INPUTS + 2 + 2 * PARTS :]
    held, (order, rates, state, sums, gather, square, turned, waiting, arrived) = (
        refs[:INPUTS], refs[INPUTS:]
    )
    copies = [
        pltpu.make_async_copy(source, target, arrived.at[i])
        for i, (source, target) in enumerate(zip(sources, held))
    ]
    for copy in copies:
        copy.start()
    recipe, eastward, northward, speed, response, photo, warmth, species = held
    n_lat, n_lon, levels, kinds = species.shape
    reactions = recipe.shape[1]
    columns = n_lat * n_lon
    chunks = reactions // 128

    flat = [counts[i // n_lon, i % n_lon] for i in range(columns)]
    for i in range(columns):
        rank = jnp.int32(0)
        for j in range(columns):
            if j != i:
                ahead = flat[j] >= flat[i] if j < i else flat[j] > flat[i]
                rank = rank + ahead.astype(jnp.int32)
        order[rank] = i

    def place(slot):
        column = order[slot]
        return column // n_lon, lax.rem(column, n_lon)

    def count_of(slot):
        a, b = place(slot)
        return counts[a, b]

    for copy in copies:
        copy.wait()
    pack_winds(eastward, northward, square, turned, packed)

    for chunk in range(chunks):
        lanes = slice(chunk * 128, (chunk + 1) * 128)
        first, second, third, fourth = [one_hot(recipe[r : r + 1, lanes], kinds) for r in range(4)]
        both = jnp.concatenate([first, second], axis=1).astype(BF)
        gather[chunk, :kinds, :] = both
        gather[chunk, kinds:, :] = both
        ends = jnp.concatenate([(third + fourth).T, (first + second).T], axis=1).astype(BF)
        sums[chunk * 256 : chunk * 256 + 128, :] = ends
        sums[chunk * 256 + 128 : chunk * 256 + 256, :] = ends

    for i in range(columns):
        a, b = place(i)
        square[i : i + 1, :levels] = warmth[a, pl.ds(b, 1), :]
    warm_columns = square[...].T
    exponent, base, light = response[...], speed[...], photo[...]
    for i in range(columns):
        a, b = place(i)
        rows = slice(i * levels, (i + 1) * levels)
        warm = jnp.broadcast_to(warm_columns[:levels, i : i + 1], (levels, reactions))
        rates[rows, :] = base * jnp.exp(exponent * warm) + light * solar[a, b]
        state[rows, :] = jnp.maximum(species[a, b], FLOOR)

    def sums_of(start, length):
        rows = slice(start * levels, (start + length) * levels)
        amounts = state[rows, :]
        picked = jnp.concatenate(split_halves(amounts), axis=1)
        flows = []
        for chunk in range(chunks):
            lanes = slice(chunk * 128, (chunk + 1) * 128)
            if chunk < chunks - SHUFFLED:
                pair = jnp.dot(picked, gather[chunk], preferred_element_type=F32)
                first, second = pair[:, :128], pair[:, 128:]
            else:
                first, second = [
                    jnp.take_along_axis(
                        amounts,
                        jnp.broadcast_to(recipe[r : r + 1, lanes], amounts.shape),
                        axis=1,
                        mode="promise_in_bounds",
                    )
                    for r in range(2)
                ]
            flows.extend(split_halves(rates[rows, lanes] * first * second))
        return jnp.dot(jnp.concatenate(flows, axis=1), sums[...], preferred_element_type=F32)

    def update(start, length, both, t, ns, steps):
        for i in range(length):
            rows = slice((start + i) * levels, (start + i + 1) * levels)
            part = slice(i * levels, (i + 1) * levels)
            amount, n, step = state[rows, :], ns[start + i], steps[start + i]
            grown = amount + step * both[part, :kinds]
            kept = amount / (amount + step * both[part, kinds:])
            state[rows, :] = jnp.where(t < n, jnp.maximum(grown * kept, FLOOR), amount)

    def run(live, begin, trips):
        half = live // 2
        ns = [count_of(i) for i in range(live)]
        steps = [1.0 / n.astype(F32) for n in ns]
        rows = slice(0, half * levels)

        @pl.when(trips > 0)
        def _():
            waiting[rows, :] = sums_of(half, half)

            def substeps(trip, carry):
                held = waiting[rows, :]
                for offset in range(UNROLL):
                    t = begin + trip * UNROLL + offset
                    both = sums_of(0, half)
                    update(half, half, held, t, ns, steps)
                    held = sums_of(half, half)
                    update(0, half, both, t, ns, steps)
                waiting[rows, :] = held
                return carry

            lax.fori_loop(0, trips, substeps, 0)

    begin = jnp.int32(0)
    for live in range(columns, 0, -group):
        trips = jnp.maximum(count_of(live - group) - begin + UNROLL - 1, 0) // UNROLL
        run(live, begin, trips)
        begin = begin + trips * UNROLL

    for i in range(columns):
        a, b = place(i)
        value = state[i * levels : (i + 1) * levels, :]
        settled[a, b] = value

        @pl.when(b > 0)
        def _():
            store_parts(to_east, (a, jnp.maximum(b - 1, 0)), value)

        @pl.when(b < n_lon - 1)
        def _():
            store_parts(to_west, (a, jnp.minimum(b, n_lon - 2)), value)


def chemistry(counts, solar, *arrays):
    recipe, eastward, species = arrays[0], arrays[1], arrays[-1]
    n_lat, n_lon, levels, kinds = species.shape
    reactions, longitudes = recipe.shape[1], eastward.shape[2]
    columns = n_lat * n_lon
    halo = pltpu.VMEM((n_lat, n_lon - 1, levels // PARTS, kinds), F32)
    return pl.pallas_call(
        functools.partial(chemistry_kernel, group=GROUP),
        out_shape=(
            pltpu.VMEM(species.shape, F32),
            jax.ShapeDtypeStruct((longitudes // n_lon, 1, 128), F32),
        )
        + (halo,) * (2 * PARTS),
        in_specs=[SMEM, SMEM] + [pl.BlockSpec(memory_space=pltpu.HBM)] * INPUTS,
        out_specs=(VMEM,) * (2 + 2 * PARTS),
        scratch_shapes=[pltpu.VMEM(array.shape, array.dtype) for array in arrays]
        + [
            pltpu.SMEM((columns,), jnp.int32),
            pltpu.VMEM((columns * levels, reactions), F32),
            pltpu.VMEM((columns * levels, kinds), F32),
            pltpu.VMEM((2 * reactions, 2 * kinds), BF),
            pltpu.VMEM((reactions // 128, 2 * kinds, 256), BF),
            pltpu.VMEM((128, 128), F32),
            pltpu.VMEM((128, 128), F32),
            pltpu.VMEM((columns * levels // 2, 2 * kinds), F32),
            pltpu.SemaphoreType.DMA((INPUTS,)),
        ],
        compiler_params=pltpu.CompilerParams(vmem_limit_bytes=60 << 20),
        cost_estimate=pl.CostEstimate(
            flops=int(2e10), bytes_accessed=2 << 20, transcendentals=0
        ),
        name="chemistry",
    )(counts, solar, *arrays)


def sweep_line(cells, faces):
    count = len(cells) - 6
    edges = {}
    for k in range(2, count + 5):
        far_left, left, right, far_right = cells[k - 2 : k + 2]
        edge = (7.0 / 12.0) * (left + right) - (1.0 / 12.0) * (far_left + far_right)
        edges[k] = jnp.minimum(
            jnp.maximum(edge, jnp.minimum(left, right)), jnp.maximum(left, right)
        )
    jumps, curves = {}, {}
    for k in range(2, count + 4):
        jumps[k] = edges[k + 1] - edges[k]
        curves[k] = 6.0 * cells[k] - 3.0 * (edges[k] + edges[k + 1])
    flux = []
    for k in range(count + 1):
        courant, at = faces[k], k + 3
        size = jnp.abs(courant)
        upwind = courant >= 0.0
        jump = jnp.where(upwind, -jumps[at - 1], jumps[at])
        curve = jnp.where(upwind, curves[at - 1], curves[at])
        value = edges[at] + 0.5 * size * (jump + (1.0 - (2.0 / 3.0) * size) * curve)
        flux.append(courant * value)
    return [cells[k + 3] - (flux[k + 1] - flux[k]) for k in range(count)]


def spread(wind, lane, tile):
    return jnp.broadcast_to(wind[:, lane : lane + 1], tile)


def wind_rows(wind, rows):
    for i in range(rows.shape[0]):
        rows[i : i + 1, :] = wind[i]
    return rows[...]


def zonal_kernel(block, wind, *refs):
    low, high = refs[:PARTS], refs[PARTS : 2 * PARTS]
    swept, inner, outer, rows = refs[2 * PARTS :]
    n_lat, n_lon = block.shape[:2]
    tile = block.shape[2:]
    winds = wind_rows(wind, rows)
    even = lax.rem(lax.axis_index("lat"), 2) == 0
    if inner.shape[0] > (n_lat - 1) * n_lon:
        inner[(n_lat - 1) * n_lon] = winds
        outer[(n_lat - 1) * n_lon] = winds
    lines = []
    for a in range(n_lat):
        cells = [load_parts(low, (a, i)) for i in range(3)]
        cells += [block[a, i] for i in range(n_lon)]
        cells += [load_parts(high, (a, i)) for i in range(3)]
        faces = [spread(winds, LANES * k + a, tile) for k in range(n_lon + 1)]
        lines.append(sweep_line(cells, faces))
        for i, value in enumerate(lines[a]):
            swept[a, i] = value
            if a > 0:
                at, below = (a - 1) * n_lon + i, lines[a - 1][i]
                inner[at] = jnp.where(even, value, below)
                outer[at] = jnp.where(even, below, value)


def meridional_kernel(block, wind, outer, inner, *refs):
    *refs, rows = refs
    first = inner.shape[0] > 3 * block.shape[1]
    if first:
        swept, passed, *sends = refs
    else:
        given, swept, sends = *refs, ()
    n_lat, n_lon = block.shape[:2]
    tile = block.shape[2:]
    band = lax.axis_index("lat")
    even = lax.rem(band, 2) == 0
    south_end, north_end = band == 0, band == lax.axis_size("lat") - 1

    def low(at):
        return jnp.where(south_end, 0.0, jnp.where(even, outer[at], inner[at]))

    def high(at):
        return jnp.where(north_end, 0.0, jnp.where(even, inner[at], outer[at]))

    winds = wind_rows(wind, rows)
    above = high(3 * n_lon) if first else given[...]
    if first:
        passed[...] = above
    for i in range(n_lon):
        cells = [low(a * n_lon + i) for a in range(3)]
        cells += [block[a, i] for a in range(n_lat)]
        cells += [high(a * n_lon + i) for a in range(3)]
        faces = [spread(winds, LANES * i + n_lat + k, tile) for k in range(n_lat)]
        faces.append(spread(above, LANES * i + n_lat, tile))
        for a, value in enumerate(sweep_line(cells, faces)):
            swept[a, i] = value
            if sends and i > 0:
                store_parts(sends[:PARTS], (a, i - 1), value)
            if sends and i < n_lon - 1:
                store_parts(sends[PARTS:], (a, i), value)


def sweep(kernel, block, wind, halos, sent_shapes, name):
    shapes = (block.shape,) + sent_shapes
    return pl.pallas_call(
        kernel,
        out_shape=tuple(jax.ShapeDtypeStruct(shape, F32) for shape in shapes),
        in_specs=[VMEM] * (2 + len(halos)),
        out_specs=(VMEM,) * len(shapes),
        scratch_shapes=[pltpu.VMEM((wind.shape[0], wind.shape[2]), F32)],
        compiler_params=pltpu.CompilerParams(vmem_limit_bytes=24 << 20),
        name=name,
    )(block, wind, *halos)


def per_device(
    species_amounts,
    thermal_anomaly,
    solar_flux_factor,
    inner_iterations,
    reference_speed,
    thermal_response,
    photo_breakup,
    reaction_recipe,
    eastward_wind_ratio,
    northward_wind_ratio,
):
    n_lat, n_lon, levels, kinds = species_amounts.shape
    lon_count, lat_count = lax.axis_size("lon"), lax.axis_size("lat")
    eastbound = [(i, (i + 1) % lon_count) for i in range(lon_count)]
    westbound = [(target, source) for source, target in eastbound]
    inner_pairs = [(i, i ^ 1) for i in range(lat_count)]
    outer_pairs = [(i, min(max(((i + 1) ^ 1) - 1, 0), lat_count - 1)) for i in range(lat_count)]

    block, packed, *sends = chemistry(
        inner_iterations,
        solar_flux_factor,
        reaction_recipe,
        eastward_wind_ratio,
        northward_wind_ratio,
        reference_speed[None],
        thermal_response[None],
        photo_breakup[None],
        thermal_anomaly,
        species_amounts,
    )
    wind = lax.all_to_all(packed, "lon", split_axis=0, concat_axis=0, tiled=True)
    zonal_halo = (n_lat, n_lon - 1, levels // PARTS, kinds)
    rows = (n_lat - 1) * n_lon
    above = ()
    for step in range(ADV_STEPS):
        halos = [
            lax.ppermute(sent, "lon", eastbound if i < PARTS else westbound)
            for i, sent in enumerate(sends)
        ]
        meridional_halo = (rows + (step == 0), levels, kinds)
        block, inner, outer = sweep(
            zonal_kernel, block, wind, halos, (meridional_halo,) * 2, "zonal"
        )
        inner = lax.ppermute(inner, "lat", inner_pairs)
        outer = lax.ppermute(outer, "lat", outer_pairs)
        sent_shapes = () if step else ((levels, 128),) + (zonal_halo,) * (2 * PARTS)
        block, *sends = sweep(
            meridional_kernel, block, wind, (outer, inner, *above), sent_shapes, "meridional"
        )
        above, sends = sends[:1], sends[1:]
    return block


def solution(mesh):
    return jax.shard_map(
        per_device,
        mesh=mesh,
        in_specs=(
            P("lat", "lon", None, None),
            P("lat", "lon", None),
            P("lat", "lon"),
            P("lat", "lon"),
            P(),
            P(),
            P(),
            P(),
            P("lon", "lat", None),
            P("lon", "lat", None),
        ),
        out_specs=P("lat", "lon", None, None),
        check_vma=False,
    )
```
